32 devices in a mesh: dp: 4 (over z), context: 2 (over x), tensor: 4 (over y, core).
Axes of the slice: x: 2, y: 2, z: 4, core: 2. Of those that a mesh axis runs over, the one named last changes fastest.
Arguments:
- hidden_in: bfloat16 [4, 512, 2048], P('dp', 'context'), may hold values from -6 to 6
- block_order: int32 [4], replicated, may hold values from 0 to 3, each once
- segment_ids: int32 [4, 512], P('dp'), may hold values from 0 to 3, never falling along the last dimension, each value on 1 to 256 neighbouring positions
- query_weight: bfloat16 [2, 2048, 2048], P(None, ('dp', 'context'), 'tensor'), may hold values from -0.125 to 0.125
- key_projection: bfloat16 [2, 2048, 1024], P(None, ('dp', 'context'), 'tensor'), may hold values from -0.125 to 0.125
- value_projection: bfloat16 [2, 2048, 1024], P(None, ('dp', 'context'), 'tensor'), may hold values from -0.125 to 0.125
- output_weight: bfloat16 [2, 2048, 2048], P(None, 'tensor', ('dp', 'context')), may hold values from -0.375 to 0.375
- gate_weight: bfloat16 [2, 2048, 6144], P(None, ('dp', 'context'), 'tensor'), may hold values from -0.125 to 0.125
- up_weight: bfloat16 [2, 2048, 6144], P(None, ('dp', 'context'), 'tensor'), may hold values from -0.125 to 0.125
- down_weight: bfloat16 [2, 6144, 2048], P(None, 'tensor', ('dp', 'context')), may hold values from -0.078125 to 0.078125
- attention_gain: bfloat16 [2, 2048], P(None, ('dp', 'context')), may hold values from 0.25 to 1.75
- mlp_gain: bfloat16 [2, 2048], P(None, ('dp', 'context')), may hold values from 0.25 to 1.75
- query_gain: bfloat16 [2, 128], P(None, ('dp', 'context')), may hold values from 0.25 to 1.75
- key_gain: bfloat16 [2, 128], P(None, ('dp', 'context')), may hold values from 0.25 to 1.75
- cotangent: bfloat16 [4, 512, 2048], P('dp', 'context'), may hold values from -6 to 6
Outputs:
- hidden_out: bfloat16 [4, 512, 2048], P('dp', 'context')
- grad_hidden: bfloat16 [4, 512, 2048], P('dp', 'context')
- grad_query: float32 [2, 2048, 2048], P(None, ('dp', 'context'), 'tensor')
- grad_key: float32 [2, 2048, 1024], P(None, ('dp', 'context'), 'tensor')
- grad_value: float32 [2, 2048, 1024], P(None, ('dp', 'context'), 'tensor')
- grad_output: float32 [2, 2048, 2048], P(None, 'tensor', ('dp', 'context'))
- grad_gate: float32 [2, 2048, 6144], P(None, ('dp', 'context'), 'tensor')
- grad_up: float32 [2, 2048, 6144], P(None, ('dp', 'context'), 'tensor')
- grad_down: float32 [2, 6144, 2048], P(None, 'tensor', ('dp', 'context'))
- grad_attention_gain: float32 [2, 2048], P(None, ('dp', 'context'))
- grad_mlp_gain: float32 [2, 2048], P(None, ('dp', 'context'))
- grad_query_gain: float32 [2, 128], P(None, ('dp', 'context'))
- grad_key_gain: float32 [2, 128], P(None, ('dp', 'context'))
The draws below stay inside these ranges and needn't reach their ends.
Inputs may be any that keep to these rules, and one draw needn't show every extreme that they name: `block_order`: each of 0 to 3 appears once. `segment_ids`: ids never fall along a sequence; each of the 4 documents spans 1 to 256 positions, one exactly that many.
All inputs are finite; a program needn't handle non-finite values.
Results may differ from the reference program's by a relative error of at most 0.035.
Values may be sent and summed in bfloat16 or wider, within the bound.
No kernel may reach another device: no remote copies, remote signals or barrier semaphores. Data moves between devices by JAX's collectives and lax.ppermute only.
A program may use at most 320 MiB of HBM per device.

```python
import math
import jax
import jax.numpy as jnp
import numpy as np
from jax import lax

MODEL_WIDTH = 2048
QUERY_HEADS = 16
KEY_VALUE_HEADS = 8
HEAD_DIM = 128
FF = 6144
DECODER_LAYERS = 2
DOCS = 4
BLOCKS = 4
SEQ_LEN = 512
SEQS = 4


def shard_levels(stream_key, extent, shards, smallest, top_value):
    level = 1.0
    for axis_at, parts in shards:
        steps = jax.random.uniform(jax.random.fold_in(jax.random.fold_in(stream_key, 6), axis_at), (parts,), jnp.float32, smallest / len(shards), top_value / len(shards))
        level = level * jnp.repeat(jnp.exp(steps), extent[axis_at] // parts).reshape((-1,) + (1,) * (len(extent) - 1 - axis_at))
    return level


def profile(number_of, total, most, lean):
    loads = [(1 << 20) // math.isqrt(grade ** lean) + 1 for grade in range(2, number_of + 1)]
    surplus, counts = total - most - (number_of - 1), [1] * (number_of - 1)
    while surplus > 0:
        candidates = [i for i in range(number_of - 1) if counts[i] < most]
        pool, left = sum([loads[i] for i in candidates]), surplus
        for i in candidates:
            addition = min(most - counts[i], max(1, left * loads[i] // pool), surplus)
            counts[i] = counts[i] + addition
            surplus = surplus - addition
    return np.array([most] + counts)


def ragged_sizes(stream_key, count, total, bound, skew):
    if count == 2:
        one = jax.random.randint(stream_key, (), max(1, total - bound), min(bound, total - 1) + 1)
        return jnp.stack([one, total - one])
    tallies = jnp.asarray(profile(count, total, bound, skew), jnp.int32)
    twos = (count - 1) // 2
    source_of, receiver = tallies[1:1 + 2 * twos:2], tallies[2:2 + 2 * twos:2]
    slack = jnp.minimum(source_of - 1, bound - receiver)
    shifted = jax.random.randint(jax.random.fold_in(stream_key, 1), (twos,), 0, 1 << 20) % (slack + 1)
    tallies = tallies.at[1:1 + 2 * twos:2].set(source_of - shifted).at[2:2 + 2 * twos:2].set(receiver + shifted)
    return tallies[jax.random.permutation(jax.random.fold_in(stream_key, 2), count)]


def gaussian(rng, shape, deviation, limit, pieces=(), held_as=jnp.bfloat16):
    drawn = deviation * jax.random.normal(rng, shape, jnp.float32)
    if pieces:
        drawn = drawn * shard_levels(rng, shape, pieces, -0.22, 0.18)
    return jnp.clip(drawn, -limit, limit).astype(held_as)


def setup_inputs(seed: int = 0) -> dict:
    arg_keys = jax.random.split(jax.random.key(seed), 16)
    return {
        "hidden_in": gaussian(arg_keys[0], (SEQS, SEQ_LEN, MODEL_WIDTH), 1.0, 6.0, ((0, 4), (1, 2))),
        "block_order": jax.random.permutation(arg_keys[1], BLOCKS).astype(jnp.int32),
        "segment_ids": jax.vmap(lambda own: jnp.searchsorted(jnp.cumsum(ragged_sizes(own, DOCS, SEQ_LEN, SEQ_LEN // 2, 0)), jnp.arange(SEQ_LEN), side="right"))(jax.random.split(arg_keys[2], SEQS)).reshape((SEQS, SEQ_LEN)).astype(jnp.int32),
        "query_weight": gaussian(arg_keys[3], (DECODER_LAYERS, MODEL_WIDTH, QUERY_HEADS * HEAD_DIM), MODEL_WIDTH ** -0.5, 0.125, ((1, 8), (2, 4))),
        "key_projection": gaussian(arg_keys[4], (DECODER_LAYERS, MODEL_WIDTH, KEY_VALUE_HEADS * HEAD_DIM), MODEL_WIDTH ** -0.5, 0.125, ((1, 8), (2, 4))),
        "value_projection": gaussian(arg_keys[5], (DECODER_LAYERS, MODEL_WIDTH, KEY_VALUE_HEADS * HEAD_DIM), MODEL_WIDTH ** -0.5, 0.125, ((1, 8), (2, 4))),
        "output_weight": gaussian(arg_keys[6], (DECODER_LAYERS, QUERY_HEADS * HEAD_DIM, MODEL_WIDTH), (QUERY_HEADS * HEAD_DIM // 8) ** -0.5, 0.375, ((1, 4), (2, 8))),
        "gate_weight": gaussian(arg_keys[7], (DECODER_LAYERS, MODEL_WIDTH, FF), MODEL_WIDTH ** -0.5, 0.125, ((1, 8), (2, 4))),
        "up_weight": gaussian(arg_keys[8], (DECODER_LAYERS, MODEL_WIDTH, FF), MODEL_WIDTH ** -0.5, 0.125, ((1, 8), (2, 4))),
        "down_weight": gaussian(arg_keys[9], (DECODER_LAYERS, FF, MODEL_WIDTH), FF ** -0.5, 0.078125, ((1, 4), (2, 8))),
        "attention_gain": jnp.clip(1.0 + 0.15 * jax.random.normal(arg_keys[10], (DECODER_LAYERS, MODEL_WIDTH), jnp.float32), 0.25, 1.75).astype(jnp.bfloat16),
        "mlp_gain": jnp.clip(1.0 + 0.15 * jax.random.normal(arg_keys[11], (DECODER_LAYERS, MODEL_WIDTH), jnp.float32), 0.25, 1.75).astype(jnp.bfloat16),
        "query_gain": jnp.clip(1.0 + 0.15 * jax.random.normal(arg_keys[12], (DECODER_LAYERS, HEAD_DIM), jnp.float32), 0.25, 1.75).astype(jnp.bfloat16),
        "key_gain": jnp.clip(1.0 + 0.15 * jax.random.normal(arg_keys[13], (DECODER_LAYERS, HEAD_DIM), jnp.float32), 0.25, 1.75).astype(jnp.bfloat16),
        "cotangent": gaussian(arg_keys[14], (SEQS, SEQ_LEN, MODEL_WIDTH), 1.0, 6.0, ((0, 4), (1, 2))),
    }


eps = 1e-06
theta = 1000000.0

def to_half(value):
    return lax.optimization_barrier(value.astype(jnp.bfloat16))

def rounded(value):
    return to_half(value).astype(jnp.float32)

def norm_rows(value, gain):
    scale = lax.rsqrt(lax.optimization_barrier(jnp.mean(value * value, axis=-1, keepdims=True)) + eps)
    return (value * scale * gain, scale)

def norm_back(value, scale, gain, grad):
    weighted = grad * gain
    inner = lax.optimization_barrier(jnp.mean(weighted * value, axis=-1, keepdims=True))
    moved = scale * weighted - value * (scale * scale * scale) * inner
    leading = tuple(range(grad.ndim - 1))
    return (moved, lax.optimization_barrier(jnp.sum(grad * value * scale, axis=leading)))

def rope_tables(positions, head_size):
    half = head_size // 2
    steps = jnp.arange(half).astype(jnp.float32) * (2.0 / head_size)
    freqs = theta ** (-steps)
    angles = positions.astype(jnp.float32)[:, None] * freqs[None, :]
    angles = jnp.concatenate([angles, angles], axis=1)
    return (jnp.cos(angles), jnp.sin(angles))

def rotate(value, cosine, sine):
    half = value.shape[-1] // 2
    turned = jnp.concatenate([-value[..., half:], value[..., :half]], axis=-1)
    return value * cosine[:, None, :] + turned * sine[:, None, :]

def rotate_back(grad, cosine, sine):
    half = grad.shape[-1] // 2
    scaled = grad * sine[:, None, :]
    turned = jnp.concatenate([scaled[..., half:], -scaled[..., :half]], axis=-1)
    return grad * cosine[:, None, :] + turned

def layout_positions(block_order, seq_len):
    block = seq_len // block_order.shape[0]
    index = jnp.arange(seq_len).astype(jnp.int32)
    return jnp.take(block_order, index // block) * block + index % block

def masked_scores(queries, keys, qpos, qseg, positions, segments):
    scores = jnp.einsum('bkgd,skd->bkgs', queries, keys) * HEAD_DIM ** (-0.5)
    allowed = (positions[None, :] <= qpos[:, None]) & (segments[None, :] == qseg[:, None])
    return jnp.where(allowed[:, None, None, :], scores, -jnp.inf)

def attention_forward(query_block, kb, value_block, positions, segments):
    row_total = query_block.shape[0]
    hidden_width = min(row_total, 512)
    token_count = row_total // hidden_width
    query_groups = QUERY_HEADS // KEY_VALUE_HEADS
    grouped_heads = query_block.reshape(token_count, hidden_width, KEY_VALUE_HEADS, query_groups, HEAD_DIM)
    qpos = positions.reshape(token_count, hidden_width)
    qseg = segments.reshape(token_count, hidden_width)
    keys = kb.astype(jnp.float32)
    values = value_block.astype(jnp.float32)

    def step(carry, item):
        block, bpos, bseg = item
        scores = masked_scores(block.astype(jnp.float32), keys, bpos, bseg, positions, segments)
        peak = lax.optimization_barrier(jnp.max(scores, axis=-1))
        logsumexp_rows = peak + jnp.log(lax.optimization_barrier(jnp.sum(jnp.exp(scores - peak[..., None]), axis=-1)))
        weights = rounded(jnp.exp(scores - logsumexp_rows[..., None]))
        attention_output = jnp.einsum('bkgs,skd->bkgd', weights, values)
        return (carry, (to_half(attention_output), logsumexp_rows))
    _, (attention_output, logsumexp_rows) = lax.scan(step, None, (grouped_heads, qpos, qseg))
    return (attention_output.reshape(row_total, QUERY_HEADS * HEAD_DIM), logsumexp_rows.reshape(row_total, KEY_VALUE_HEADS, query_groups))

def attention_backward(query_block, kb, value_block, output_block_flat, logsumexp_rows, output_gradient_block, positions, segments):
    row_total = query_block.shape[0]
    hidden_width = min(row_total, 512)
    token_count = row_total // hidden_width
    query_groups = QUERY_HEADS // KEY_VALUE_HEADS
    grouped_heads = query_block.reshape(token_count, hidden_width, KEY_VALUE_HEADS, query_groups, HEAD_DIM)
    upstream_gradient = output_gradient_block.reshape(token_count, hidden_width, KEY_VALUE_HEADS, query_groups, HEAD_DIM)
    output_delta = lax.optimization_barrier(jnp.sum(output_block_flat.astype(jnp.float32).reshape(row_total, KEY_VALUE_HEADS, query_groups, HEAD_DIM) * output_gradient_block.astype(jnp.float32).reshape(row_total, KEY_VALUE_HEADS, query_groups, HEAD_DIM), axis=-1))
    output_delta = output_delta.reshape(token_count, hidden_width, KEY_VALUE_HEADS, query_groups)
    logsumexp_blocks = logsumexp_rows.reshape(token_count, hidden_width, KEY_VALUE_HEADS, query_groups)
    qpos = positions.reshape(token_count, hidden_width)
    qseg = segments.reshape(token_count, hidden_width)
    keys = kb.astype(jnp.float32)
    values = value_block.astype(jnp.float32)

    def step(carry, item):
        d_keys, value_gradient = carry
        block, bpos, bseg, grad_block, block_lse, block_delta = item
        queries = block.astype(jnp.float32)
        scores = masked_scores(queries, keys, bpos, bseg, positions, segments)
        probs = jnp.exp(scores - block_lse[..., None])
        weights = rounded(probs)
        grads = grad_block.astype(jnp.float32)
        d_probs = jnp.einsum('bkgd,skd->bkgs', grads, values)
        d_scores = rounded(HEAD_DIM ** (-0.5) * probs * (d_probs - block_delta[..., None]))
        d_query = jnp.einsum('bkgs,skd->bkgd', d_scores, keys)
        d_keys = d_keys + jnp.einsum('bkgs,bkgd->skd', d_scores, queries)
        value_gradient = value_gradient + jnp.einsum('bkgs,bkgd->skd', weights, grads)
        return ((d_keys, value_gradient), d_query)
    zero_scalar = jnp.zeros((row_total, KEY_VALUE_HEADS, HEAD_DIM), jnp.float32)
    (d_keys, value_gradient), d_query = lax.scan(step, (zero_scalar, zero_scalar), (grouped_heads, qpos, qseg, upstream_gradient, logsumexp_blocks, output_delta))
    return (d_query.reshape(row_total, QUERY_HEADS, HEAD_DIM), d_keys, value_gradient)

def layer_forward(state, params, cosine, sine, positions, segments):
    wq, key_matrix, value_matrix, wo, wg, wu, wd, g_attn, g_mlp, g_query, g_key = params
    row_total = state.shape[0]
    normed, scale_one = norm_rows(state, g_attn.astype(jnp.float32))
    hidden_first = normed.astype(jnp.bfloat16)
    q_raw = jnp.dot(hidden_first, wq, preferred_element_type=jnp.float32).reshape(row_total, QUERY_HEADS, HEAD_DIM)
    key_unrotated = jnp.dot(hidden_first, key_matrix, preferred_element_type=jnp.float32).reshape(row_total, KEY_VALUE_HEADS, HEAD_DIM)
    q_normed, q_scale = norm_rows(q_raw, g_query.astype(jnp.float32))
    k_normed, k_scale = norm_rows(key_unrotated, g_key.astype(jnp.float32))
    query_block = rotate(q_normed, cosine, sine).astype(jnp.bfloat16)
    kb = rotate(k_normed, cosine, sine).astype(jnp.bfloat16)
    value_block = jnp.dot(hidden_first, value_matrix, preferred_element_type=jnp.float32).astype(jnp.bfloat16).reshape(row_total, KEY_VALUE_HEADS, HEAD_DIM)
    output_block_flat, logsumexp_rows = attention_forward(query_block, kb, value_block, positions, segments)
    mid = state + jnp.dot(output_block_flat, wo, preferred_element_type=jnp.float32)
    normed_two, scale_two = norm_rows(mid, g_mlp.astype(jnp.float32))
    h_two = normed_two.astype(jnp.bfloat16)
    gate = jnp.dot(h_two, wg, preferred_element_type=jnp.float32)
    upper = jnp.dot(h_two, wu, preferred_element_type=jnp.float32)
    hidden = (jax.nn.silu(gate) * upper).astype(jnp.bfloat16)
    result = mid + jnp.dot(hidden, wd, preferred_element_type=jnp.float32)
    keep = (state, scale_one, hidden_first, q_raw, q_scale, key_unrotated, k_scale, query_block, kb, value_block, output_block_flat, logsumexp_rows, mid, scale_two, h_two, gate, upper, hidden)
    return (result, keep)

def layer_backward(grad, params, keep, cosine, sine, positions, segments):
    wq, key_matrix, value_matrix, wo, wg, wu, wd, g_attn, g_mlp, g_query, g_key = params
    state, scale_one, hidden_first, q_raw, q_scale, key_unrotated, k_scale, query_block, kb, value_block, output_block_flat, logsumexp_rows, mid, scale_two, h_two, gate, upper, hidden = keep
    row_total = grad.shape[0]
    grad_half = grad.astype(jnp.bfloat16)
    d_hidden = jnp.dot(grad_half, wd.T, preferred_element_type=jnp.float32)
    d_down = jnp.dot(hidden.T, grad_half, preferred_element_type=jnp.float32)
    sig = jax.nn.sigmoid(gate)
    d_gate = (d_hidden * upper * sig * (1.0 + gate * (1.0 - sig))).astype(jnp.bfloat16)
    d_upper = (d_hidden * gate * sig).astype(jnp.bfloat16)
    d_gate_w = jnp.dot(h_two.T, d_gate, preferred_element_type=jnp.float32)
    d_up_w = jnp.dot(h_two.T, d_upper, preferred_element_type=jnp.float32)
    d_h_two = jnp.dot(d_gate, wg.T, preferred_element_type=jnp.float32) + jnp.dot(d_upper, wu.T, preferred_element_type=jnp.float32)
    d_mid, d_g_mlp = norm_back(mid, scale_two, g_mlp.astype(jnp.float32), d_h_two)
    d_mid = grad + d_mid
    mid_half = d_mid.astype(jnp.bfloat16)
    output_gradient_block = to_half(jnp.dot(mid_half, wo.T, preferred_element_type=jnp.float32))
    d_out_w = jnp.dot(output_block_flat.T, mid_half, preferred_element_type=jnp.float32)
    d_query, d_keys, value_gradient = attention_backward(query_block, kb, value_block, output_block_flat, logsumexp_rows, output_gradient_block, positions, segments)
    dq_raw, d_g_query = norm_back(q_raw, q_scale, g_query.astype(jnp.float32), rotate_back(d_query, cosine, sine))
    key_gradient_full, d_g_key = norm_back(key_unrotated, k_scale, g_key.astype(jnp.float32), rotate_back(d_keys, cosine, sine))
    dq_half = dq_raw.reshape(row_total, QUERY_HEADS * HEAD_DIM).astype(jnp.bfloat16)
    key_gradient_half = key_gradient_full.reshape(row_total, KEY_VALUE_HEADS * HEAD_DIM).astype(jnp.bfloat16)
    value_gradient_half = value_gradient.reshape(row_total, KEY_VALUE_HEADS * HEAD_DIM).astype(jnp.bfloat16)
    d_wq = jnp.dot(hidden_first.T, dq_half, preferred_element_type=jnp.float32)
    d_wk = jnp.dot(hidden_first.T, key_gradient_half, preferred_element_type=jnp.float32)
    d_wv = jnp.dot(hidden_first.T, value_gradient_half, preferred_element_type=jnp.float32)
    d_h_one = jnp.dot(dq_half, wq.T, preferred_element_type=jnp.float32) + jnp.dot(key_gradient_half, key_matrix.T, preferred_element_type=jnp.float32) + jnp.dot(value_gradient_half, value_matrix.T, preferred_element_type=jnp.float32)
    d_state, d_g_attn = norm_back(state, scale_one, g_attn.astype(jnp.float32), d_h_one)
    return (d_mid + d_state, (d_wq, d_wk, d_wv, d_out_w, d_gate_w, d_up_w, d_down, d_g_attn, d_g_mlp, d_g_query, d_g_key))

def reference(hidden_in, block_order, segment_ids, query_weight, key_projection, value_projection, output_weight, gate_weight, up_weight, down_weight, attention_gain, mlp_gain, query_gain, key_gain, cotangent):
    positions = layout_positions(block_order, SEQ_LEN)
    cosine, sine = rope_tables(positions, HEAD_DIM)
    weights = (query_weight, key_projection, value_projection, output_weight, gate_weight, up_weight, down_weight, attention_gain, mlp_gain, query_gain, key_gain)

    def one_sequence(totals, item):
        tokens, seg_row, upstream_gradient = item
        segments = jnp.take(seg_row, positions)
        state = tokens.astype(jnp.float32)
        saved = []
        for layer in range(DECODER_LAYERS):
            params = tuple((w[layer] for w in weights))
            state, keep = layer_forward(state, params, cosine, sine, positions, segments)
            saved.append(keep)
        result = state.astype(jnp.bfloat16)
        grad = upstream_gradient.astype(jnp.float32)
        layer_grads = [None] * DECODER_LAYERS
        for layer in reversed(range(DECODER_LAYERS)):
            params = tuple((w[layer] for w in weights))
            grad, layer_grads[layer] = layer_backward(grad, params, saved[layer], cosine, sine, positions, segments)
        stacked = tuple((jnp.stack([layer_grads[l][i] for l in range(DECODER_LAYERS)]) for i in range(11)))
        totals = tuple((a + b for a, b in zip(totals, stacked)))
        return (totals, (result, grad.astype(jnp.bfloat16)))
    zero_array = tuple((jnp.zeros(w.shape, jnp.float32) for w in weights))
    totals, (outputs, grads_in) = lax.scan(one_sequence, zero_array, (hidden_in, segment_ids, cotangent))
    return (outputs, grads_in, totals[0], totals[1], totals[2], totals[3], totals[4], totals[5], totals[6], totals[7], totals[8], totals[9], totals[10])
```

```python
import jax
import jax.numpy as jnp
from jax import lax
from jax.sharding import PartitionSpec as P

AXES = ("dp", "context", "tensor")
DP = 4
LAYERS = 2
EPS = 1e-06
THETA = 1000000.0


def nt(a, b):
    return lax.dot_general(a, b, (((1,), (1,)), ((), ())), preferred_element_type=jnp.float32)


def nn(a, b):
    return lax.dot_general(a, b, (((1,), (0,)), ((), ())), preferred_element_type=jnp.float32)


def tn(a, b):
    return lax.dot_general(a, b, (((0,), (0,)), ((), ())), preferred_element_type=jnp.float32)


def half(v):
    return v.astype(jnp.bfloat16)


def full(v):
    return v.astype(jnp.float32)


def norm_scale(v):
    return lax.rsqrt(jnp.mean(v * v, axis=-1, keepdims=True) + EPS)


def norm_back(v, scale, gain, grad):
    weighted = grad * gain
    inner = jnp.mean(weighted * v, axis=-1, keepdims=True)
    moved = scale * weighted - v * (scale * scale * scale) * inner
    return moved, jnp.sum(grad * v * scale, axis=0)


def rotate(v, cosine, sine):
    h = v.shape[-1] // 2
    turned = jnp.concatenate([-v[:, h:], v[:, :h]], axis=-1)
    return v * cosine + turned * sine


def rotate_back(e, cosine, sine):
    h = e.shape[-1] // 2
    scaled = e * sine
    turned = jnp.concatenate([scaled[:, h:], -scaled[:, :h]], axis=-1)
    return e * cosine + turned


class Step:
    def __init__(self, mesh):
        self.C = mesh.shape["context"]
        self.G = self.C // 2
        assert mesh.shape["dp"] == DP and mesh.shape["tensor"] == 4 and self.C % 2 == 0
        ids = [(d, c, y, k) for d in range(DP) for c in range(self.C) for y in range(2) for k in range(2)]
        self.ids = ids

    def flat(self, p):
        d, c, y, k = p
        return ((d * self.C + c) * 2 + y) * 2 + k

    def send(self, x, move):
        return lax.ppermute(x, AXES, [(self.flat(p), self.flat(move(*p))) for p in self.ids])

    def over_z(self, x, s):
        return self.send(x, lambda d, c, y, k: (d ^ s, c, y, k))

    def over_c(self, x, u):
        return self.send(x, lambda d, c, y, k: (d, c ^ u, y, k))

    def over_y(self, x):
        return self.send(x, lambda d, c, y, k: (d, c, y ^ 1, k))

    def over_k(self, x):
        return self.send(x, lambda d, c, y, k: (d, c, y, k ^ 1))

    def over_group(self, x, e):
        def move(d, c, y, k):
            g = (2 * c + y) ^ e
            return d, g // 2, g % 2, k

        return self.send(x, move)

    def to_group(self, d, c, y, k):
        g = d * self.G + c // 2
        return 2 * (c % 2) + y, g // 2, g % 2, k

    def xor_axis(self, v, axis, index):
        size, bit = v.shape[axis], 1
        while bit < size:
            shape = v.shape
            split = v.reshape(shape[:axis] + (size // (2 * bit), 2, bit) + shape[axis + 1 :])
            flipped = jnp.flip(split, axis + 1)
            v = jnp.where((index // bit) % 2 == 1, flipped, split).reshape(shape)
            bit *= 2
        return v

    def width_to_group(self, v):
        rows, width = v.shape
        v = v.reshape(rows, DP, self.C, 2, width // (DP * self.C * 2))
        v = self.xor_axis(self.xor_axis(v, 2, self.c), 3, self.y)
        return v.transpose(0, 2, 3, 1, 4).reshape(rows, width)

    def width_from_group(self, v):
        rows, width = v.shape
        v = v.reshape(rows, self.C, 2, DP, width // (DP * self.C * 2))
        v = self.xor_axis(self.xor_axis(v, 1, self.c), 2, self.y)
        return v.transpose(0, 3, 1, 2, 4).reshape(rows, width)

    def spread(self, blocks):
        rows = blocks[0].shape[0]
        parts = [jnp.concatenate([b[:, j * (b.shape[1] // 2) : (j + 1) * (b.shape[1] // 2)] for b in blocks], axis=1) for j in (0, 1)]
        local = jnp.stack(parts)
        n = local.shape[2]
        local = local.reshape(2, 2, rows // 2, n)
        kept = lax.dynamic_index_in_dim(local, self.y, 1, keepdims=False)
        other = self.over_y(lax.dynamic_index_in_dim(local, 1 - self.y, 1, keepdims=False))
        first = self.y == 0
        by_rank = jnp.concatenate([jnp.where(first, kept, other), jnp.where(first, other, kept)])
        piece = jnp.zeros((DP, rows // 2, n), jnp.bfloat16)
        for s in range(DP):
            mine = lax.dynamic_index_in_dim(by_rank, self.d ^ s, 0, keepdims=True)
            if s:
                mine = self.over_z(mine, s)
            piece = lax.dynamic_update_slice_in_dim(piece, mine, self.d ^ s, 0)
        piece = piece.reshape(DP * rows // 2, n)
        out = []
        beside = self.over_y(piece)
        for u in range(self.C):
            if u == 0:
                out += [piece, beside]
            else:
                out += [self.over_c(piece, u), self.over_c(beside, u)]
        return jnp.concatenate(out)

    def collect(self, grad):
        width, n = grad.shape
        grad = grad.reshape(self.C, 2, width // (2 * self.C), n)
        here, beside = full(grad[0, 0]), full(grad[0, 1])
        for u in range(1, self.C):
            here = here + full(self.over_c(grad[u, 0], u))
            beside = beside + full(self.over_c(grad[u, 1], u))
        total = half(here + full(self.over_y(half(beside))))
        total = total.reshape(DP, width // (2 * self.C * DP), n)
        by_rank = jnp.zeros_like(total)
        for s in range(DP):
            mine = lax.dynamic_index_in_dim(total, self.d ^ s, 0, keepdims=True)
            if s:
                mine = self.over_z(mine, s)
            by_rank = lax.dynamic_update_slice_in_dim(by_rank, mine, self.d ^ s, 0)
        pair = by_rank.reshape(2, 2, total.shape[1], n)
        kept = lax.dynamic_index_in_dim(pair, self.y, 0, keepdims=False)
        other = self.over_y(lax.dynamic_index_in_dim(pair, 1 - self.y, 0, keepdims=False))
        first = self.y == 0
        both = jnp.concatenate([jnp.where(first, kept, other), jnp.where(first, other, kept)], axis=1)
        return full(both)

    def gather_rows(self, shard):
        own = [shard] + [self.over_z(shard, s) for s in range(1, DP)]
        return jnp.concatenate(own + [self.over_k(v) for v in own])

    def scatter_rows(self, part):
        rows = part.shape[0] // 2
        size = rows // DP
        mine = part[:rows] + full(self.over_k(half(part[rows:])))
        total = mine[:size]
        sent = half(mine[size:])
        for s in range(1, DP):
            total = total + full(self.over_z(sent[(s - 1) * size : s * size], s))
        return total

    def keys_of_group(self, v):
        return jnp.concatenate([v] + [self.over_group(v, e) for e in range(1, self.G)]) if self.G > 1 else v

    def sum_to_group(self, v):
        rows = v.shape[0] // self.G
        total = v[:rows]
        for e in range(1, self.G):
            total = total + full(self.over_group(half(v[e * rows : (e + 1) * rows]), e))
        return total

    def scores(self, q, k):
        return jnp.where(self.allowed, nt(q, k) * q.shape[1] ** (-0.5), -jnp.inf)

    def body(
        self,
        hidden_in,
        block_order,
        segment_ids,
        query_weight,
        key_projection,
        value_projection,
        output_weight,
        gate_weight,
        up_weight,
        down_weight,
        attention_gain,
        mlp_gain,
        query_gain,
        key_gain,
        cotangent,
    ):
        self.d, self.c = lax.axis_index("dp"), lax.axis_index("context")
        tensor = lax.axis_index("tensor")
        self.y, self.k = tensor // 2, tensor % 2
        d, c, y, k = self.d, self.c, self.y, self.k
        C, G = self.C, self.G
        head = query_gain.shape[1] * DP * C
        rows, width = hidden_in.shape[1:]
        size = rows // 4
        seq_len = C * rows
        group = 2 * c + y

        small = jnp.concatenate(
            [attention_gain.reshape(-1), mlp_gain.reshape(-1), query_gain.reshape(-1), key_gain.reshape(-1), half(segment_ids.reshape(-1))]
        )[None]
        small = jnp.concatenate([small] + [self.over_z(small, s) for s in range(1, DP)])
        small = jnp.stack([small] + [self.over_c(small, u) for u in range(1, C)], axis=1)
        small = self.xor_axis(self.xor_axis(small, 0, d), 1, c)
        at, parts = 0, []
        for v in (attention_gain, mlp_gain, query_gain, key_gain):
            part = full(small[:, :, at : at + v.size]).reshape(DP, C, LAYERS, v.shape[1])
            parts.append(part.transpose(2, 0, 1, 3).reshape(LAYERS, -1))
            at += v.size
        gain_one, gain_two, gain_query, gain_key = parts
        gain_one, gain_two = self.width_to_group(gain_one), self.width_to_group(gain_two)
        segments = lax.dynamic_index_in_dim(small[:, 0, at:], group // G, 0, keepdims=False).astype(jnp.int32)

        def places(which):
            shard = 2 * (d ^ jnp.arange(DP))[None, :] + (k ^ jnp.arange(2))[:, None]
            return (which * 8 * size + shard[:, :, None] * size + jnp.arange(size)).reshape(-1)

        block = seq_len // block_order.shape[0]

        def positions(which):
            at = places(which)
            return jnp.take(block_order, at // block) * block + at % block

        within = group % G
        qpos = positions(within)
        kpos = jnp.concatenate([positions(within ^ e) for e in range(G)])
        qseg, kseg = jnp.take(segments, qpos), jnp.take(segments, kpos)
        self.allowed = (kpos[None, :] <= qpos[:, None]) & (kseg[None, :] == qseg[:, None])
        steps = jnp.arange(head // 2).astype(jnp.float32) * (2.0 / head)
        angles = qpos.astype(jnp.float32)[:, None] * (THETA ** (-steps))[None, :]
        angles = jnp.concatenate([angles, angles], axis=1)
        cosine, sine = jnp.cos(angles), jnp.sin(angles)

        def to_shard(v):
            mine = lax.dynamic_slice_in_dim(v[0], tensor * size, size)
            return full(self.width_to_group(self.send(mine, self.to_group)))

        x = to_shard(hidden_in)
        grad = to_shard(cotangent)

        weights = []
        for l in range(LAYERS):
            att = self.spread([query_weight[l], key_projection[l], value_projection[l], output_weight[l].T])
            gu = self.spread([gate_weight[l], up_weight[l]])
            dn = self.spread([down_weight[l].T])
            weights.append((att, gu, dn))
        scale = head ** (-0.5)

        kept = []
        for l in range(LAYERS):
            att_w, gu_w, dn_w = weights[l]
            wqkv, wo = att_w[:, : 4 * head], att_w[:, 4 * head :]
            s1 = norm_scale(x)
            h1 = self.gather_rows(half(x * s1 * gain_one[l]))
            raw = nn(h1, wqkv)
            q_raw = [raw[:, i * head : (i + 1) * head] for i in (0, 1)]
            k_raw = raw[:, 2 * head : 3 * head]
            q_s, k_s = [norm_scale(v) for v in q_raw], norm_scale(k_raw)
            qh = [half(rotate(v * s * gain_query[l], cosine, sine)) for v, s in zip(q_raw, q_s)]
            kh = self.keys_of_group(half(rotate(k_raw * k_s * gain_key[l], cosine, sine)))
            vh = self.keys_of_group(half(raw[:, 3 * head :]))
            lse, heads = [], []
            for q in qh:
                sc = self.scores(q, kh)
                peak = jnp.max(sc, axis=-1, keepdims=True)
                lse.append(peak + jnp.log(jnp.sum(jnp.exp(sc - peak), axis=-1, keepdims=True)))
                heads.append(half(nn(half(jnp.exp(sc - lse[-1])), vh)))
            att = jnp.concatenate(heads, axis=1)
            mid = x + self.scatter_rows(nt(att, wo))
            s2 = norm_scale(mid)
            h2 = self.gather_rows(half(mid * s2 * gain_two[l]))
            both = nn(h2, gu_w)
            ff = both.shape[1] // 2
            gate, up = both[:, :ff], both[:, ff:]
            hid = half(gate * jax.nn.sigmoid(gate) * up)
            kept.append((x, s1, h1, q_raw, k_raw, q_s, k_s, qh, kh, vh, lse, heads, att, mid, s2, h2, gate, up, hid))
            x = mid + self.scatter_rows(nt(hid, dn_w))

        def from_shard(v):
            inverse = {self.to_group(*p): p for p in self.ids}
            v = self.send(half(self.width_from_group(v)), lambda *p: inverse[p])
            v = jnp.stack([v, self.over_k(v)])
            v = jnp.stack([v, self.over_y(v)])
            v = self.xor_axis(self.xor_axis(v, 0, y), 1, k)
            return v.reshape(1, rows, width)

        hidden_out = from_shard(x)

        grads = [None] * LAYERS
        gains = [None] * LAYERS
        for l in reversed(range(LAYERS)):
            att_w, gu_w, dn_w = weights[l]
            wqkv, wo = att_w[:, : 4 * head], att_w[:, 4 * head :]
            x, s1, h1, q_raw, k_raw, q_s, k_s, qh, kh, vh, lse, heads, att, mid, s2, h2, gate, up, hid = kept[l]
            cb = self.gather_rows(half(grad))
            d_hid = nn(cb, dn_w)
            d_dn = half(tn(cb, hid))
            sig = jax.nn.sigmoid(gate)
            d_gate = half(d_hid * up * sig * (1.0 + gate * (1.0 - sig)))
            d_up = half(d_hid * gate * sig)
            d_both = jnp.concatenate([d_gate, d_up], axis=1)
            d_h2 = self.scatter_rows(nt(d_both, gu_w))
            d_gu = half(tn(h2, d_both))
            moved, g_two = norm_back(mid, s2, gain_two[l], d_h2)
            d_mid = grad + moved
            yb = self.gather_rows(half(d_mid))
            d_att = half(nn(yb, wo))
            d_wo = half(tn(yb, att))
            dq, dk, dv = [], 0.0, 0.0
            for i in (0, 1):
                e = d_att[:, i * head : (i + 1) * head]
                delta = jnp.sum(full(e) * full(heads[i]), axis=-1, keepdims=True)
                probs = jnp.exp(self.scores(qh[i], kh) - lse[i])
                d_sc = half(scale * probs * (nt(e, vh) - delta))
                dq.append(nn(d_sc, kh))
                dk = dk + tn(d_sc, qh[i])
                dv = dv + tn(half(probs), e)
            dk, dv = self.sum_to_group(dk), self.sum_to_group(dv)
            backs = [norm_back(v, s, gain_query[l], rotate_back(e, cosine, sine)) for v, s, e in zip(q_raw, q_s, dq)]
            k_back, g_key = norm_back(k_raw, k_s, gain_key[l], rotate_back(dk, cosine, sine))
            d_qkv = jnp.concatenate([half(v) for v in (backs[0][0], backs[1][0], k_back, dv)], axis=1)
            d_h1 = self.scatter_rows(nt(d_qkv, wqkv))
            d_wqkv = half(tn(h1, d_qkv))
            moved, g_one = norm_back(x, s1, gain_one[l], d_h1)
            grad = d_mid + moved
            grads[l] = tuple(self.collect(v) for v in (d_dn, d_gu, d_wo, d_wqkv))
            gains[l] = jnp.concatenate(
                [self.width_from_group(g_one[None])[0], self.width_from_group(g_two[None])[0], backs[0][1] + backs[1][1], g_key]
            )
        grad_hidden = from_shard(grad)

        total = jnp.stack(gains)
        bit = 1
        while bit < C:
            total = total + self.over_c(total, bit)
            bit *= 2
        for s in (1, 2):
            total = total + self.over_z(total, s)
        total = total + self.over_y(total)
        total = total + self.over_k(total)
        at = d * C + c
        outs_gain, start = [], 0
        for v, n in ((attention_gain, width), (mlp_gain, width), (query_gain, head), (key_gain, head)):
            outs_gain.append(lax.dynamic_slice_in_dim(total[:, start : start + n], at * v.shape[1], v.shape[1], axis=1))
            start += n

        def rowed(v):
            return jnp.concatenate([v[0], v[1]], axis=1)

        def stacked(f):
            return jnp.stack([f(grads[l]) for l in range(LAYERS)])

        ff = gate_weight.shape[2] // 2
        return (
            hidden_out,
            grad_hidden,
            stacked(lambda g: rowed(g[3][:, :, : 2 * head])),
            stacked(lambda g: rowed(g[3][:, :, 2 * head : 3 * head])),
            stacked(lambda g: rowed(g[3][:, :, 3 * head :])),
            stacked(lambda g: rowed(g[2]).T),
            stacked(lambda g: rowed(g[1][:, :, :ff])),
            stacked(lambda g: rowed(g[1][:, :, ff:])),
            stacked(lambda g: rowed(g[0]).T),
            *outs_gain,
        )


def solution(mesh):
    step = Step(mesh)
    weight_in = P(None, ("dp", "context"), "tensor")
    weight_out = P(None, "tensor", ("dp", "context"))
    gain = P(None, ("dp", "context"))
    stream = P("dp", "context", None)
    return jax.shard_map(
        step.body,
        mesh=mesh,
        in_specs=(stream, P(), P("dp", None))
        + (weight_in, weight_in, weight_in, weight_out, weight_in, weight_in, weight_out)
        + (gain, gain, gain, gain, stream),
        out_specs=(stream, stream)
        + (weight_in, weight_in, weight_in, weight_out, weight_in, weight_in, weight_out)
        + (gain, gain, gain, gain),
        check_vma=False,
    )
```
